32 devices in a mesh: grp: 2 (over y), win: 4 (over z), uly: 4 (over x, core).
Axes of the slice: x: 2, y: 2, z: 4, core: 2. Of those that a mesh axis runs over, the one named last changes fastest.
Arguments:
- query_rows: bfloat16 [8, 16, 64, 5120], P(('grp', 'win'), None, 'uly'), parts along dimension 0, may hold values from -140 to 140
- key_rows: bfloat16 [8, 16, 64, 5120], P(('grp', 'win'), None, 'uly'), parts along dimension 0, may hold values from -140 to 140
- value_rows: bfloat16 [8, 16, 64, 5120], P(('grp', 'win'), None, 'uly'), parts along dimension 0, may hold values from -6 to 6
- query_gain: float32 [5120], replicated, may hold values from 0.25 to 1.75
- key_gain: float32 [5120], replicated, may hold values from 0.25 to 1.75
- window_start: int32 [8], P('grp'), parts along dimension 0, may hold values from 0 to 40, as said below
- owner_of_phase: int32 [8], P('grp'), parts along dimension 0, may hold values from 0 to 3, each once
- blend_weight: int32 [8, 16], P('grp'), parts along dimension 0, may hold values from 1 to 8
Outputs:
- owned_frames: bfloat16 [96, 64, 5120], P(('grp', 'win'), 'uly'), parts along dimension 0
- next_windows: bfloat16 [8, 16, 64, 5120], P(('grp', 'win'), None, 'uly'), parts along dimension 0
The draws below stay inside these ranges and needn't reach their ends.
There are 2 independent parts, one for each index of `grp`. The reference program is written for one: setup_inputs(seed, part) draws one part's arguments, and reference() takes and returns one part's arrays. A program takes and returns all parts, laid end to end along the dimension named above; an argument that names none is the same for every part. Nothing has to cross between parts.
Inputs may be any that keep to these rules, and one draw needn't show every extreme that they name: `window_start`: window w starts at frame w * 12 plus an offset of 0 to 4; in some pair of consecutive windows (the last one followed by the first counts as consecutive) the first offset is 4 and the second 0. `owner_of_phase`: a permutation.
All inputs are finite; a program needn't handle non-finite values.
Results may differ from the reference program's by a relative error of at most 0.0015.
The reference program's roundings to bfloat16 on the way count: a program that leaves them out, or rounds other values in their place, can miss the bound.
Values may be sent and summed in bfloat16 or wider, within the bound.
A program may use at most 128 MiB of HBM per device.

```python
import math
import jax
import jax.numpy as jnp
from jax import lax

D = 5120
HEADS = 40
HD = 128
P_SIZE = 64
WF = 16
FR = 12
SHIFT = 6
NW = 4
FRAMES = 48


def shared_layout(key):
    column_scale = jnp.exp(jax.random.uniform(jax.random.fold_in(key, 11), (D,), jnp.float32) * math.log(10.0))
    return column_scale


def draw_query_rows(key, part):
    column_scale = shared_layout(key)
    own_key = jax.random.fold_in(key, 21)
    drawn = jnp.clip(jax.random.normal(own_key, (NW, WF, P_SIZE, D), jnp.float32), -6.0, 6.0) * column_scale
    return drawn.astype(jnp.bfloat16)


def draw_key_rows(key, part):
    column_scale = shared_layout(key)
    own_key = jax.random.fold_in(key, 31)
    drawn = jnp.clip(jax.random.normal(own_key, (NW, WF, P_SIZE, D), jnp.float32), -6.0, 6.0) * column_scale
    return drawn.astype(jnp.bfloat16)


def draw_window_start(key, part):
    offsets = jax.random.randint(jax.random.fold_in(key, 41), (NW,), 0, WF - FR + 1)
    chosen = jax.random.randint(jax.random.fold_in(key, 42), (), 0, NW)
    window_index = jnp.arange(NW)
    offsets = jnp.where(window_index == chosen, WF - FR, offsets)
    offsets = jnp.where(window_index == (chosen + 1) % NW, 0, offsets)
    return (window_index * FR + offsets).astype(jnp.int32)


def plant(entries, rng, least, high):
    extent = entries.shape
    place = [jax.random.randint(jax.random.fold_in(rng, axis), (), 0, extent[axis]) for axis in range(len(extent))]
    entries = entries.at[tuple(place)].set(least)
    longest = extent.index(max(extent))
    place[longest] = (place[longest] + 1) % extent[longest]
    return entries.at[tuple(place)].set(high)


def levels(rng, extent, shards, least, largest):
    def one(dim, parts):
        draws = jax.random.uniform(jax.random.fold_in(jax.random.fold_in(rng, 6), dim), (parts,), jnp.float32, least / len(shards), largest / len(shards))
        return jnp.repeat(jnp.exp(draws), extent[dim] // parts).reshape((-1,) + (1,) * (len(extent) - dim - 1))

    loudness = one(*shards[0])
    for cut in shards[1:]:
        loudness = loudness * one(*cut)
    return loudness


def noise(stream_key, shape, scale, reach, pieces=(), held_as=jnp.bfloat16):
    entries = scale * jax.random.normal(stream_key, shape, jnp.float32)
    if pieces:
        entries = entries * levels(stream_key, shape, pieces, -0.22, 0.18)
    return jnp.clip(entries, -reach, reach).astype(held_as)


def setup_inputs(seed: int = 0, part: int = 0) -> dict:
    key_list = jax.random.split(jax.random.key(seed), 9)
    own_keys = jax.random.split(jax.random.fold_in(key_list[8], part), 9)
    query_rows = draw_query_rows(jax.random.fold_in(jax.random.fold_in(key_list[8], part), 71), part)
    key_rows = draw_key_rows(jax.random.fold_in(jax.random.fold_in(key_list[8], part), 71), part)
    value_rows = noise(own_keys[2], (NW, WF, P_SIZE, D), 1.0, 6.0, ((0, 4), (2, 4)))
    query_gain = jnp.clip(1.0 + 0.15 * jax.random.normal(key_list[3], (D,), jnp.float32), 0.25, 1.75)
    key_gain = jnp.clip(1.0 + 0.15 * jax.random.normal(key_list[4], (D,), jnp.float32), 0.25, 1.75)
    window_start = draw_window_start(jax.random.fold_in(jax.random.fold_in(key_list[8], part), 71), part)
    owner_of_phase = jax.random.permutation(own_keys[6], NW).astype(jnp.int32)
    blend_weight = plant(jax.random.randint(own_keys[7], (NW, WF), 1, 9), jax.random.fold_in(own_keys[7], 1), 1, 8).astype(jnp.int32)
    return dict(query_rows=query_rows, key_rows=key_rows, value_rows=value_rows, query_gain=query_gain, key_gain=key_gain, window_start=window_start, owner_of_phase=owner_of_phase, blend_weight=blend_weight)


def normalize(row_block, gain_vector):
    floats = row_block.astype(jnp.float32)
    mean_square = lax.optimization_barrier(jnp.mean(floats * floats, axis=-1, keepdims=True))
    return (floats * lax.rsqrt(mean_square + 1e-06) * gain_vector).astype(jnp.bfloat16)

def head_attention(operands):
    query_head, key_head, value_head = operands
    scores = jnp.dot(query_head, key_head.T, preferred_element_type=jnp.float32) * (1.0 / math.sqrt(query_head.shape[-1]))
    row_max = lax.optimization_barrier(jnp.max(scores, axis=-1, keepdims=True))
    exponent = jnp.exp(scores - row_max)
    weights = (exponent / lax.optimization_barrier(jnp.sum(exponent, axis=-1, keepdims=True))).astype(jnp.bfloat16)
    return jnp.dot(weights, value_head, preferred_element_type=jnp.float32).astype(jnp.bfloat16)

def reference(query_rows, key_rows, value_rows, query_gain, key_gain, window_start, owner_of_phase, blend_weight):
    token_count = WF * P_SIZE

    def split_heads(tensor):
        return jnp.moveaxis(tensor.reshape(token_count, HEADS, HD), 1, 0)

    def window_attention(operands):
        query_win, key_win, value_win = operands
        result = lax.map(head_attention, (split_heads(normalize(query_win, query_gain)), split_heads(normalize(key_win, key_gain)), split_heads(value_win)))
        return jnp.moveaxis(result, 0, 1).reshape(WF, P_SIZE, D)
    window_out = lax.map(window_attention, (query_rows, key_rows, value_rows))
    frame_range = jnp.arange(WF, dtype=jnp.int32)
    frame_of = ((window_start[:, None] + frame_range[None, :]) % FRAMES).reshape(-1).astype(jnp.int32)
    weight_float = blend_weight.astype(jnp.float32)
    terms = (weight_float[:, :, None, None] * window_out.astype(jnp.float32)).reshape(NW * WF, P_SIZE, D)
    numerator = jnp.zeros((FRAMES, P_SIZE, D), jnp.float32).at[frame_of].add(terms)
    denominator = jnp.zeros((FRAMES,), jnp.float32).at[frame_of].add(weight_float.reshape(-1))
    blended = (numerator / denominator[:, None, None]).astype(jnp.bfloat16)
    phase_range = jnp.arange(NW, dtype=jnp.int32)
    inverse = jnp.zeros((NW,), jnp.int32).at[owner_of_phase].set(phase_range)
    owned_index = (jnp.arange(FR, dtype=jnp.int32)[None, :] * NW + inverse[:, None]).reshape(-1).astype(jnp.int32)
    owned_frames = blended[owned_index]
    next_index = ((window_start[:, None] + SHIFT + frame_range[None, :]) % FRAMES).reshape(-1).astype(jnp.int32)
    next_windows = blended[next_index].reshape(NW, WF, P_SIZE, D)
    return (owned_frames, next_windows)
```

```python
import functools
import math

import jax
import jax.numpy as jnp
from jax import lax
from jax.experimental import pallas as pl
from jax.experimental.pallas import tpu as pltpu
from jax.sharding import PartitionSpec as P

HEADS = 40
WF = 16
FR = 12
HALO = WF - FR
SHIFT = FR // 2
AHEAD = HALO + SHIFT
CHUNKS = 4
LAG_BLEND = 1
LAG_RETURN = 1
LAG_LAST = 2
ROWS = 16


def fused(
    dims,
    start_ref,
    owner_ref,
    weight_ref,
    q_ref,
    k_ref,
    v_ref,
    qg_ref,
    kg_ref,
    owned_ref,
    next_ref,
    q_now,
    k_now,
    root,
    stage,
    inbox,
    vbox,
    attended,
    halo_in,
    halo_now,
    x_out,
    x_in,
    r_out,
    r_in,
    n_in,
    pool,
    inverse,
    near_at,
    near_w,
    far_at,
    far_w,
    give_at,
    owned_at,
    q_send,
    q_recv,
    k_send,
    k_recv,
    v_send,
    v_recv,
    ho_send,
    ho_recv,
    xo_send,
    xo_recv,
    ro_send,
    ro_recv,
    no_send,
    no_recv,
    q_load,
    k_load,
):
    ulysses, windows, share, given, steps, head, tokens = dims
    local = tokens // WF
    me = lax.axis_index("uly")
    my_window = lax.axis_index("win")
    below = lax.rem(my_window + windows - 1, windows)
    above = lax.rem(my_window + 1, windows)

    def peer(d):
        return lax.rem(me + d, ulysses)

    def far(d):
        return lax.rem(my_window + d, windows)

    def given_slots(d):
        return (0, 1) if d == 1 else (1 + (d - 2) * share, share)

    chunk = tokens // CHUNKS

    def load(ref, now, sem, c):
        rows = pl.ds(pl.multiple_of(c * chunk, chunk), chunk)
        return pltpu.make_async_copy(ref.at[rows], now.at[rows], sem.at[c])

    for ref, now, sem in ((q_ref, q_now, q_load), (k_ref, k_now, k_load)):
        for c in range(CHUNKS):
            load(ref, now, sem, c).start()

    barrier = pltpu.get_barrier_semaphore()
    for d in range(1, ulysses):
        pl.semaphore_signal(
            barrier, inc=1, device_id={"uly": peer(d)}, device_id_type=pl.DeviceIdType.MESH
        )
    for d in range(1, windows):
        pl.semaphore_signal(
            barrier, inc=1, device_id={"win": far(d)}, device_id_type=pl.DeviceIdType.MESH
        )

    def remote(source, target, send, recv, axis, to):
        pltpu.make_async_remote_copy(
            src_ref=source,
            dst_ref=target,
            send_sem=send,
            recv_sem=recv,
            device_id={axis: to},
            device_id_type=pl.DeviceIdType.MESH,
        ).start()

    def spread(source, target, send, recv):
        for d in range(1, ulysses):
            to = peer(d)
            remote(source(to), target(me), send, recv, "uly", to)
        pltpu.make_async_copy(source(me), target(me), recv).start()

    def arrived(ref, sem):
        pltpu.make_async_copy(ref, ref, sem).wait()

    def columns(u, s):
        return pl.ds(pl.multiple_of((u * steps + s) * head, head), head)

    def scale_columns(which, s):
        now, gain = ((q_now, qg_ref), (k_now, kg_ref))[which]
        for u in range(ulysses):
            at = columns(u, s)
            scaled = now[:, at].astype(jnp.float32) * root[which] * gain[:, at]
            stage[which, u, s] = scaled.astype(jnp.bfloat16)

    def send_values(s):
        spread(
            lambda u: v_ref.at[:, columns(u, s)],
            lambda u: vbox.at[s, u],
            v_send.at[s],
            v_recv.at[s],
        )

    def send_scored(which, s):
        spread(
            lambda u: stage.at[which, u, s],
            lambda u: inbox.at[which, s, u],
            (q_send, k_send)[which].at[s],
            (q_recv, k_recv)[which].at[s],
        )

    frames_total = FR * windows

    def tables():
        def invert(o, carry):
            def seek(phase, found):
                return jnp.where(owner_ref[phase] == o, phase, found)

            inverse[o] = lax.fori_loop(0, windows, seek, jnp.int32(0))
            return carry

        lax.fori_loop(0, windows, invert, 0)
        my_phase = inverse[my_window]
        first = FR * my_window + HALO

        def per_owner(o, carry):
            rest = lax.rem(inverse[o] - first + frames_total, windows)
            for c in range(share):
                give_at[o * share + c] = jnp.minimum(rest + c * windows, FR - 1)
            return carry

        lax.fori_loop(0, windows, per_owner, 0)
        rest = lax.rem(inverse[below] - first + frames_total, windows)
        extra = jnp.int32(AHEAD)
        for f in range(AHEAD, FR):
            extra = jnp.where(rest == f % windows, f, extra)
        give_at[below * share] = extra


        def offset_of(w):
            return jnp.clip(start_ref[w] - FR * w, 0, HALO)

        offset = offset_of(my_window)
        offset_below = offset_of(below)
        offset_above = offset_of(above)
        for f in range(FR):
            own = f + HALO - offset
            near_at[f] = own
            near_w[f] = weight_ref[my_window, own].astype(jnp.float32)
            if f < HALO:
                at = f + WF - offset_below
                held = at < WF
                at = jnp.minimum(at, WF - 1)
                far_at[f] = at - FR
                far_w[f] = jnp.where(held, weight_ref[below, at], 0).astype(jnp.float32)
            elif f >= FR - HALO:
                at = f - (FR - HALO) - offset_above
                held = at >= 0
                at = jnp.maximum(at, 0)
                far_at[f] = at + HALO
                far_w[f] = jnp.where(held, weight_ref[above, at], 0).astype(jnp.float32)
        for f in range(FR):
            place = lax.rem(f * windows + my_phase - HALO + frames_total, frames_total)
            home = place // FR
            at = place - home * FR
            apart = lax.rem(home - my_window + windows, windows)
            given_at = FR + AHEAD + 1 + (apart - 2) * share + at // windows
            ahead = FR + jnp.minimum(at, AHEAD)
            owned_at[f] = jnp.where(
                home == my_window, at, jnp.where(home == above, ahead, given_at)
            )
        return offset + SHIFT - HALO

    for which, (ref, now, sem, gain) in enumerate(
        ((q_ref, q_now, q_load, qg_ref), (k_ref, k_now, k_load, kg_ref))
    ):

        def norm_block(t, carry, which=which, ref=ref, now=now, sem=sem, gain=gain):
            blocks = chunk // ROWS

            @pl.when(lax.rem(t, blocks) == 0)
            def _():
                load(ref, now, sem, t // blocks).wait()

            rows = pl.ds(pl.multiple_of(t * ROWS, ROWS), ROWS)
            floats = now[rows, :].astype(jnp.float32)
            mean_square = jnp.mean(floats * floats, axis=-1, keepdims=True)
            root[which, rows, :] = jnp.broadcast_to(
                lax.rsqrt(mean_square + 1e-06), (ROWS, head)
            )
            return carry

        lax.fori_loop(0, tokens // ROWS, norm_block, 0)
        scale_columns(which, 0)

    pl.semaphore_wait(barrier, ulysses + windows - 2)

    send_scored(0, 0)
    send_scored(1, 0)
    send_values(0)
    for which in range(2):
        scale_columns(which, 1)
    send_values(1)

    next_at = tables()

    scale = 1.0 / math.sqrt(head)

    def attention(s):
        arrived(inbox.at[0, s], q_recv.at[s])
        arrived(inbox.at[1, s], k_recv.at[s])
        arrived(vbox.at[s], v_recv.at[s])

        @pl.when(s + 1 < steps)
        def _():
            send_scored(0, s + 1)
            send_scored(1, s + 1)

        @pl.when(s + 2 < steps)
        def _():
            send_values(s + 2)

        keys = inbox[1, s].reshape(ulysses * tokens, head)
        values = vbox[s].reshape(ulysses * tokens, head)
        for u in range(ulysses):
            scores = (
                lax.dot_general(
                    inbox[0, s, u],
                    keys,
                    (((1,), (1,)), ((), ())),
                    preferred_element_type=jnp.float32,
                )
                * scale
            )
            exponent = jnp.exp(scores - jnp.max(scores, axis=-1, keepdims=True))
            inverse_sum = 1.0 / jnp.sum(exponent, axis=-1, keepdims=True)
            weights = (exponent * inverse_sum).astype(jnp.bfloat16)
            result = jnp.dot(weights, values, preferred_element_type=jnp.float32)
            attended[s, :, u] = result.astype(jnp.bfloat16).reshape(WF, local, head)
        remote(
            attended.at[s, pl.ds(0, HALO)],
            halo_in.at[s, 1],
            ho_send.at[s],
            ho_recv.at[s],
            "win",
            below,
        )
        remote(
            attended.at[s, pl.ds(FR, HALO)],
            halo_in.at[s, 0],
            ho_send.at[s],
            ho_recv.at[s],
            "win",
            above,
        )

        @pl.when(s + 2 < steps)
        def _():
            for which in range(2):
                scale_columns(which, s + 2)

    def blend(s):
        arrived(halo_in.at[s], ho_recv.at[s])
        for side in range(2):
            halo_now[side * HALO : (side + 1) * HALO] = halo_in[s, side]
        for f in range(FR):
            numerator = near_w[f] * attended[s, near_at[f]].astype(jnp.float32)
            denominator = near_w[f]
            if f < HALO or f >= FR - HALO:
                numerator += far_w[f] * halo_now[far_at[f]].astype(jnp.float32)
                denominator += far_w[f]
            x_out[s, :, f] = (numerator / denominator).astype(jnp.bfloat16)
        spread(
            lambda u: x_out.at[s, u],
            lambda u: x_in.at[s, u],
            xo_send.at[s],
            xo_recv.at[s],
        )

    def give_back(s):
        arrived(x_in.at[s], xo_recv.at[s])
        remote(
            x_in.at[s, :, pl.ds(0, AHEAD)],
            n_in.at[s],
            no_send.at[s],
            no_recv.at[s],
            "win",
            below,
        )
        for f in range(FR):
            pool[f] = x_in[s, :, f]
        for d in range(1, windows):
            o = far(d)
            base, count = given_slots(windows - d)
            for c in range(count):
                r_out[s, base + c] = pool[give_at[o * share + c]]
            many = pl.ds(base, count)
            remote(
                r_out.at[s, many], r_in.at[s, many], ro_send.at[s], ro_recv.at[s], "win", o
            )

    def finish(s):
        arrived(n_in.at[s], no_recv.at[s])
        arrived(r_in.at[s], ro_recv.at[s])
        for f in range(FR):
            pool[f] = x_in[s, :, f]
        for f in range(AHEAD):
            pool[FR + f] = n_in[s, :, f]
        for c in range(given):
            pool[FR + AHEAD + c] = r_in[s, c]
        for f in range(FR):
            frame = pool[owned_at[f]]
            for u in range(ulysses):
                owned_ref[f, :, columns(u, s)] = frame[u]
        for j in range(WF):
            frame = pool[next_at + j]
            for u in range(ulysses):
                next_ref[j, :, columns(u, s)] = frame[u]

    def step(i, carry):
        for lag, work in (
            (LAG_BLEND, blend),
            (0, attention),
            (LAG_RETURN, give_back),
            (LAG_LAST, finish),
        ):

            @pl.when((i >= lag) & (i < steps + lag))
            def _(lag=lag, work=work):
                work(i - lag)

        return carry

    lax.fori_loop(0, steps + LAG_LAST, step, 0)

    def sent(s, carry):
        arrived(inbox.at[0, s, pl.ds(0, ulysses - 1)], q_send.at[s])
        arrived(inbox.at[1, s, pl.ds(0, ulysses - 1)], k_send.at[s])
        arrived(vbox.at[s, pl.ds(0, ulysses - 1)], v_send.at[s])
        arrived(halo_in.at[s], ho_send.at[s])
        arrived(x_out.at[s, pl.ds(0, ulysses - 1)], xo_send.at[s])
        arrived(n_in.at[s], no_send.at[s])
        arrived(r_in.at[s], ro_send.at[s])
        return carry

    lax.fori_loop(0, steps, sent, 0)


def per_device(
    query_rows,
    key_rows,
    value_rows,
    query_gain,
    key_gain,
    window_start,
    owner_of_phase,
    blend_weight,
):
    windows = lax.axis_size("win")
    ulysses = lax.axis_size("uly")
    share = (FR + windows - 1) // windows
    given = 1 + (windows - 2) * share
    local = query_rows.shape[2]
    features = query_rows.shape[3]
    head = features // HEADS
    steps = HEADS // ulysses
    tokens = WF * local
    smem = pl.BlockSpec(memory_space=pltpu.SMEM)
    vmem = pl.BlockSpec(memory_space=pltpu.VMEM)
    hbm = pl.BlockSpec(memory_space=pl.ANY)
    bf16 = jnp.bfloat16
    sems = pltpu.SemaphoreType.DMA((steps,))
    frame = (ulysses, local, head)
    owned, next_rows = pl.pallas_call(
        functools.partial(fused, (ulysses, windows, share, given, steps, head, tokens)),
        out_shape=(
            pltpu.VMEM((FR, local, features), bf16),
            pltpu.VMEM((WF, local, features), bf16),
        ),
        in_specs=[smem] * 3 + [hbm] * 3 + [vmem] * 2,
        out_specs=(vmem, vmem),
        scratch_shapes=[
            pltpu.VMEM((tokens, features), bf16),
            pltpu.VMEM((tokens, features), bf16),
            pltpu.VMEM((2, tokens, head), jnp.float32),
            pltpu.VMEM((2, ulysses, steps, tokens, head), bf16),
            pltpu.VMEM((2, steps, ulysses, tokens, head), bf16),
            pltpu.VMEM((steps, ulysses, tokens, head), bf16),
            pltpu.VMEM((steps, WF) + frame, bf16),
            pltpu.VMEM((steps, 2, HALO) + frame, bf16),
            pltpu.VMEM((2 * HALO,) + frame, bf16),
            pltpu.VMEM((steps, ulysses, FR, local, head), bf16),
            pltpu.VMEM((steps, ulysses, FR, local, head), bf16),
            pltpu.VMEM((steps, given) + frame, bf16),
            pltpu.VMEM((steps, given) + frame, bf16),
            pltpu.VMEM((steps, ulysses, AHEAD, local, head), bf16),
            pltpu.VMEM((FR + AHEAD + given,) + frame, bf16),
            pltpu.SMEM((windows,), jnp.int32),
            pltpu.SMEM((FR,), jnp.int32),
            pltpu.SMEM((FR,), jnp.float32),
            pltpu.SMEM((FR,), jnp.int32),
            pltpu.SMEM((FR,), jnp.float32),
            pltpu.SMEM((windows * share,), jnp.int32),
            pltpu.SMEM((FR,), jnp.int32),
        ]
        + [sems] * 14
        + [pltpu.SemaphoreType.DMA((CHUNKS,))] * 2,
        compiler_params=pltpu.CompilerParams(
            collective_id=0, has_side_effects=True, vmem_limit_bytes=62 * 1000 * 1000
        ),
    )(
        window_start,
        owner_of_phase,
        blend_weight,
        query_rows.reshape(tokens, features),
        key_rows.reshape(tokens, features),
        value_rows.reshape(tokens, features),
        query_gain.reshape(1, features),
        key_gain.reshape(1, features),
    )
    return (owned, next_rows[None])


def solution(mesh):
    placed = (
        P(("grp", "win"), None, "uly", None),
        P(("grp", "win"), None, "uly", None),
        P(("grp", "win"), None, "uly", None),
        P(),
        P(),
        P("grp"),
        P("grp"),
        P("grp", None),
    )
    return jax.shard_map(
        per_device,
        mesh=mesh,
        in_specs=placed,
        out_specs=(P(("grp", "win"), "uly", None), P(("grp", "win"), None, "uly", None)),
        check_vma=False,
    )
```

```python
import functools
import math

import jax
import jax.numpy as jnp
from jax import lax
from jax.experimental import pallas as pl
from jax.experimental.pallas import tpu as pltpu
from jax.sharding import PartitionSpec as P

HEADS = 40
WF = 16
FR = 12
HALO = WF - FR
SHIFT = FR // 2
AHEAD = HALO + SHIFT
CHUNKS = 4
LAG_BLEND = 1
LAG_RETURN = 1
LAG_LAST = 2
ROWS = 16


def fused(
    dims,
    start_ref,
    owner_ref,
    weight_ref,
    q_ref,
    k_ref,
    v_ref,
    qg_ref,
    kg_ref,
    owned_ref,
    next_ref,
    q_now,
    k_now,
    root,
    stage,
    inbox,
    vbox,
    attended,
    halo_in,
    halo_now,
    x_out,
    x_in,
    r_out,
    r_in,
    n_in,
    pool,
    raw_out,
    raw_in,
    blended,
    rl_out,
    rl_in,
    inverse,
    near_at,
    near_w,
    far_at,
    far_w,
    give_at,
    owned_at,
    q_send,
    q_recv,
    k_send,
    k_recv,
    v_send,
    v_recv,
    ho_send,
    ho_recv,
    xo_send,
    xo_recv,
    ro_send,
    ro_recv,
    no_send,
    no_recv,
    raw_send,
    raw_recv,
    n_last,
    r_last,
    q_load,
    k_load,
):
    ulysses, windows, share, given, steps, head, tokens = dims
    local = tokens // WF
    me = lax.axis_index("uly")
    my_window = lax.axis_index("win")
    below = lax.rem(my_window + windows - 1, windows)
    above = lax.rem(my_window + 1, windows)

    def peer(d):
        return lax.rem(me + d, ulysses)

    def far(d):
        return lax.rem(my_window + d, windows)

    def near_first(d):
        if ulysses % 2:
            return peer(d)
        pair = lax.rem(lax.div(me, 2) + d // 2, ulysses // 2)
        return pair * 2 + lax.rem(me + d, 2)

    def given_slots(d):
        return (0, 1) if d == 1 else (1 + (d - 2) * share, share)

    chunk = tokens // CHUNKS

    def load(ref, now, sem, c):
        rows = pl.ds(pl.multiple_of(c * chunk, chunk), chunk)
        return pltpu.make_async_copy(ref.at[rows], now.at[rows], sem.at[c])

    for ref, now, sem in ((q_ref, q_now, q_load), (k_ref, k_now, k_load)):
        for c in range(CHUNKS):
            load(ref, now, sem, c).start()

    barrier = pltpu.get_barrier_semaphore()
    for d in range(1, ulysses):
        pl.semaphore_signal(
            barrier, inc=1, device_id={"uly": peer(d)}, device_id_type=pl.DeviceIdType.MESH
        )
    for d in range(1, windows):
        pl.semaphore_signal(
            barrier, inc=1, device_id={"win": far(d)}, device_id_type=pl.DeviceIdType.MESH
        )

    def remote(source, target, send, recv, to):
        pltpu.make_async_remote_copy(
            src_ref=source,
            dst_ref=target,
            send_sem=send,
            recv_sem=recv,
            device_id=to,
            device_id_type=pl.DeviceIdType.MESH,
        ).start()

    def spread(source, target, send, recv):
        for d in range(1, ulysses):
            to = near_first(d)
            remote(source(to), target(me), send, recv, {"uly": to})
        pltpu.make_async_copy(source(me), target(me), recv).start()

    def arrived(ref, sem):
        pltpu.make_async_copy(ref, ref, sem).wait()

    def columns(u, s):
        return pl.ds(pl.multiple_of((u * steps + s) * head, head), head)

    def scale_columns(which, s):
        now, gain = ((q_now, qg_ref), (k_now, kg_ref))[which]
        for u in range(ulysses):
            at = columns(u, s)
            scaled = now[:, at].astype(jnp.float32) * root[which] * gain[:, at]
            stage[which, u, s] = scaled.astype(jnp.bfloat16)

    def send_values(s):
        spread(
            lambda u: v_ref.at[:, columns(u, s)],
            lambda u: vbox.at[s, u],
            v_send.at[s],
            v_recv.at[s],
        )

    def send_scored(which, s):
        spread(
            lambda u: stage.at[which, u, s],
            lambda u: inbox.at[which, s, u],
            (q_send, k_send)[which].at[s],
            q_recv.at[s, me] if which == 0 else k_recv.at[s],
        )

    frames_total = FR * windows

    def tables():
        def invert(o, carry):
            def seek(phase, found):
                return jnp.where(owner_ref[phase] == o, phase, found)

            inverse[o] = lax.fori_loop(0, windows, seek, jnp.int32(0))
            return carry

        lax.fori_loop(0, windows, invert, 0)
        my_phase = inverse[my_window]
        first = FR * my_window + HALO

        def per_owner(o, carry):
            rest = lax.rem(inverse[o] - first + frames_total, windows)
            for c in range(share):
                give_at[o * share + c] = jnp.minimum(rest + c * windows, FR - 1)
            return carry

        lax.fori_loop(0, windows, per_owner, 0)
        rest = lax.rem(inverse[below] - first + frames_total, windows)
        extra = jnp.int32(AHEAD)
        for f in range(AHEAD, FR):
            extra = jnp.where(rest == f % windows, f, extra)
        give_at[below * share] = extra


        def offset_of(w):
            return jnp.clip(start_ref[w] - FR * w, 0, HALO)

        offset = offset_of(my_window)
        offset_below = offset_of(below)
        offset_above = offset_of(above)
        for f in range(FR):
            own = f + HALO - offset
            near_at[f] = own
            near_w[f] = weight_ref[my_window, own].astype(jnp.float32)
            if f < HALO:
                at = f + WF - offset_below
                held = at < WF
                at = jnp.minimum(at, WF - 1)
                far_at[f] = at - FR
                far_w[f] = jnp.where(held, weight_ref[below, at], 0).astype(jnp.float32)
            elif f >= FR - HALO:
                at = f - (FR - HALO) - offset_above
                held = at >= 0
                at = jnp.maximum(at, 0)
                far_at[f] = at + HALO
                far_w[f] = jnp.where(held, weight_ref[above, at], 0).astype(jnp.float32)
        for f in range(FR):
            place = lax.rem(f * windows + my_phase - HALO + frames_total, frames_total)
            home = place // FR
            at = place - home * FR
            apart = lax.rem(home - my_window + windows, windows)
            given_at = FR + AHEAD + 1 + (apart - 2) * share + at // windows
            ahead = FR + jnp.minimum(at, AHEAD)
            owned_at[f] = jnp.where(
                home == my_window, at, jnp.where(home == above, ahead, given_at)
            )
        return offset + SHIFT - HALO

    for which, (ref, now, sem, gain) in enumerate(
        ((q_ref, q_now, q_load, qg_ref), (k_ref, k_now, k_load, kg_ref))
    ):

        def norm_block(t, carry, which=which, ref=ref, now=now, sem=sem, gain=gain):
            blocks = chunk // ROWS

            @pl.when(lax.rem(t, blocks) == 0)
            def _():
                load(ref, now, sem, t // blocks).wait()

            rows = pl.ds(pl.multiple_of(t * ROWS, ROWS), ROWS)
            floats = now[rows, :].astype(jnp.float32)
            mean_square = jnp.mean(floats * floats, axis=-1, keepdims=True)
            root[which, rows, :] = jnp.broadcast_to(
                lax.rsqrt(mean_square + 1e-06), (ROWS, head)
            )
            return carry

        lax.fori_loop(0, tokens // ROWS, norm_block, 0)
        scale_columns(which, 0)

    pl.semaphore_wait(barrier, ulysses + windows - 2)

    send_scored(1, 0)
    send_values(0)
    send_scored(0, 0)
    for which in range(2):
        scale_columns(which, 1)

    next_at = tables()

    scale = 1.0 / math.sqrt(head)

    def attend(s, then):
        keys = inbox[1, s].reshape(ulysses * tokens, head)
        values = vbox[s].reshape(ulysses * tokens, head)
        for d in range(ulysses):
            u = near_first(d)
            arrived(inbox.at[0, s, u], q_recv.at[s, u])
            scores = (
                lax.dot_general(
                    inbox[0, s, u],
                    keys,
                    (((1,), (1,)), ((), ())),
                    preferred_element_type=jnp.float32,
                )
                * scale
            )
            exponent = jnp.exp(scores - jnp.max(scores, axis=-1, keepdims=True))
            inverse_sum = 1.0 / jnp.sum(exponent, axis=-1, keepdims=True)
            weights = (exponent * inverse_sum).astype(jnp.bfloat16)
            result = jnp.dot(weights, values, preferred_element_type=jnp.float32)
            then(u, result.astype(jnp.bfloat16).reshape(WF, local, head))

    def both_halos(halo_below, halo_above):
        pl.when(my_window > 0)(halo_below)
        halo_above()
        pl.when(my_window == 0)(halo_below)

    def attention(s):
        arrived(inbox.at[1, s], k_recv.at[s])
        arrived(vbox.at[s], v_recv.at[s])
        send_scored(1, s + 1)
        send_values(s + 1)
        send_scored(0, s + 1)

        def keep(u, result):
            attended[s, :, u] = result

        attend(s, keep)

        def send(side, at, to):
            return lambda: remote(
                attended.at[s, pl.ds(at, HALO)],
                halo_in.at[s, side],
                ho_send.at[s],
                ho_recv.at[s],
                {"win": to},
            )

        both_halos(send(1, 0, below), send(0, FR, above))

        @pl.when(s + 2 < steps)
        def _():
            for which in range(2):
                scale_columns(which, s + 2)

    def blend(s):
        arrived(halo_in.at[s], ho_recv.at[s])
        for side in range(2):
            halo_now[side * HALO : (side + 1) * HALO] = halo_in[s, side]
        for f in range(FR):
            numerator = near_w[f] * attended[s, near_at[f]].astype(jnp.float32)
            denominator = near_w[f]
            if f < HALO or f >= FR - HALO:
                numerator += far_w[f] * halo_now[far_at[f]].astype(jnp.float32)
                denominator += far_w[f]
            x_out[s, :, f] = (numerator / denominator).astype(jnp.bfloat16)
        spread(
            lambda u: x_out.at[s, u],
            lambda u: x_in.at[s, u],
            xo_send.at[s],
            xo_recv.at[s],
        )

    def to_all(give):
        for d in range(1, windows):

            @pl.when(my_window + d < windows)
            def _(d=d):
                give(my_window + d, windows - d)

            @pl.when(my_window >= d)
            def _(d=d):
                give(my_window - d, d)

    def give_back(s):
        arrived(x_in.at[s], xo_recv.at[s])
        for f in range(FR):
            pool[f] = x_in[s, :, f]

        def give(o, apart):
            base, count = given_slots(apart)
            for c in range(count):
                r_out[s, base + c] = pool[give_at[o * share + c]]
            many = pl.ds(base, count)
            remote(
                r_out.at[s, many], r_in.at[s, many], ro_send.at[s], ro_recv.at[s], {"win": o}
            )
            if apart == 1:
                remote(
                    x_in.at[s, :, pl.ds(0, AHEAD)],
                    n_in.at[s],
                    no_send.at[s],
                    no_recv.at[s],
                    {"win": o},
                )

        to_all(give)

    def finish(s):
        arrived(n_in.at[s], no_recv.at[s])
        arrived(r_in.at[s], ro_recv.at[s])
        for f in range(FR):
            pool[f] = x_in[s, :, f]
        for f in range(AHEAD):
            pool[FR + f] = n_in[s, :, f]
        for c in range(given):
            pool[FR + AHEAD + c] = r_in[s, c]
        for f in range(FR):
            frame = pool[owned_at[f]]
            for u in range(ulysses):
                owned_ref[f, :, columns(u, s)] = frame[u]
        for j in range(WF):
            frame = pool[next_at + j]
            for u in range(ulysses):
                next_ref[j, :, columns(u, s)] = frame[u]

    last = steps - 1

    def last_attention():
        arrived(inbox.at[1, last], k_recv.at[last])
        arrived(vbox.at[last], v_recv.at[last])

        def give_raw(u, result):
            raw_out[u] = result

            def send(side, at, to):
                return lambda: remote(
                    raw_out.at[u, pl.ds(at, HALO)],
                    raw_in.at[me, pl.ds(FR + side * HALO, HALO)],
                    raw_send.at[u],
                    raw_recv.at[me],
                    {"win": to, "uly": u},
                )

            both_halos(send(1, 0, below), send(0, FR, above))
            for f in range(FR):
                x_out[last, u, f] = raw_out[u, near_at[f]]
            home = raw_in.at[me, pl.ds(0, FR)]

            @pl.when(u != me)
            def _():
                remote(x_out.at[last, u], home, xo_send.at[last], raw_recv.at[me], {"uly": u})

            @pl.when(u == me)
            def _():
                pltpu.make_async_copy(x_out.at[last, u], home, raw_recv.at[me]).start()

        attend(last, give_raw)

    def last_blend():
        for d in range(ulysses):
            m = near_first(d)
            arrived(raw_in.at[m], raw_recv.at[m])
            for f in range(2 * HALO):
                halo_now[f, 0] = raw_in[m, FR + f]
            for f in range(FR):
                numerator = near_w[f] * raw_in[m, f].astype(jnp.float32)
                denominator = near_w[f]
                if f < HALO or f >= FR - HALO:
                    numerator += far_w[f] * halo_now[far_at[f], 0].astype(jnp.float32)
                    denominator += far_w[f]
                blended[m, f] = (numerator / denominator).astype(jnp.bfloat16)

            def give(o, apart):
                base, count = given_slots(apart)
                for c in range(count):
                    rl_out[m, base + c] = blended[m, give_at[o * share + c]]
                many = pl.ds(base, count)
                remote(
                    rl_out.at[m, many],
                    rl_in.at[m, many],
                    ro_send.at[last],
                    r_last.at[m],
                    {"win": o},
                )
                if apart == 1:
                    remote(
                        blended.at[m, pl.ds(0, AHEAD)],
                        n_in.at[last, m],
                        no_send.at[last],
                        n_last.at[m],
                        {"win": o},
                    )

            to_all(give)

    def last_finish():
        for d in range(ulysses):
            m = near_first(d)
            arrived(n_in.at[last, m], n_last.at[m])
            arrived(rl_in.at[m], r_last.at[m])
            for f in range(FR):
                pool[f, 0] = blended[m, f]
            for f in range(AHEAD):
                pool[FR + f, 0] = n_in[last, m, f]
            for c in range(given):
                pool[FR + AHEAD + c, 0] = rl_in[m, c]
            at = columns(m, last)
            for f in range(FR):
                owned_ref[f, :, at] = pool[owned_at[f], 0]
            for j in range(WF):
                next_ref[j, :, at] = pool[next_at + j, 0]

    def step(i, carry):
        for lag, work in (
            (LAG_BLEND, blend),
            (0, attention),
            (LAG_RETURN, give_back),
            (LAG_LAST, finish),
        ):

            @pl.when((i >= lag) & (i < last + lag))
            def _(lag=lag, work=work):
                work(i - lag)

        return carry

    lax.fori_loop(0, last, step, 0)
    blend(last - 1)
    last_attention()
    give_back(last - 1)
    finish(last - 2)
    last_blend()
    finish(last - 1)
    last_finish()

    def sent(s, carry):
        arrived(inbox.at[0, s, pl.ds(0, ulysses - 1)], q_send.at[s])
        arrived(inbox.at[1, s, pl.ds(0, ulysses - 1)], k_send.at[s])
        arrived(vbox.at[s, pl.ds(0, ulysses - 1)], v_send.at[s])
        arrived(x_out.at[s, pl.ds(0, ulysses - 1)], xo_send.at[s])
        arrived(n_in.at[s], no_send.at[s])
        arrived(r_in.at[s], ro_send.at[s])
        return carry

    lax.fori_loop(0, steps, sent, 0)

    def halo_sent(s, carry):
        arrived(halo_in.at[s], ho_send.at[s])
        return carry

    lax.fori_loop(0, last, halo_sent, 0)
    for u in range(ulysses):
        arrived(raw_in.at[u, pl.ds(FR, 2 * HALO)], raw_send.at[u])


def per_device(
    query_rows,
    key_rows,
    value_rows,
    query_gain,
    key_gain,
    window_start,
    owner_of_phase,
    blend_weight,
):
    windows = lax.axis_size("win")
    ulysses = lax.axis_size("uly")
    share = (FR + windows - 1) // windows
    given = 1 + (windows - 2) * share
    local = query_rows.shape[2]
    features = query_rows.shape[3]
    head = features // HEADS
    steps = HEADS // ulysses
    tokens = WF * local
    smem = pl.BlockSpec(memory_space=pltpu.SMEM)
    vmem = pl.BlockSpec(memory_space=pltpu.VMEM)
    hbm = pl.BlockSpec(memory_space=pl.ANY)
    bf16 = jnp.bfloat16
    sems = pltpu.SemaphoreType.DMA((steps,))
    frame = (ulysses, local, head)
    owned, next_rows = pl.pallas_call(
        functools.partial(fused, (ulysses, windows, share, given, steps, head, tokens)),
        out_shape=(
            pltpu.VMEM((FR, local, features), bf16),
            pltpu.VMEM((WF, local, features), bf16),
        ),
        in_specs=[smem] * 3 + [hbm] * 3 + [vmem] * 2,
        out_specs=(vmem, vmem),
        scratch_shapes=[
            pltpu.VMEM((tokens, features), bf16),
            pltpu.VMEM((tokens, features), bf16),
            pltpu.VMEM((2, tokens, head), jnp.float32),
            pltpu.VMEM((2, ulysses, steps, tokens, head), bf16),
            pltpu.VMEM((2, steps, ulysses, tokens, head), bf16),
            pltpu.VMEM((steps, ulysses, tokens, head), bf16),
            pltpu.VMEM((steps, WF) + frame, bf16),
            pltpu.VMEM((steps, 2, HALO) + frame, bf16),
            pltpu.VMEM((2 * HALO,) + frame, bf16),
            pltpu.VMEM((steps, ulysses, FR, local, head), bf16),
            pltpu.VMEM((steps, ulysses, FR, local, head), bf16),
            pltpu.VMEM((steps, given) + frame, bf16),
            pltpu.VMEM((steps, given) + frame, bf16),
            pltpu.VMEM((steps, ulysses, AHEAD, local, head), bf16),
            pltpu.VMEM((FR + AHEAD + given,) + frame, bf16),
            pltpu.VMEM((ulysses, WF, local, head), bf16),
            pltpu.VMEM((ulysses, FR + 2 * HALO, local, head), bf16),
            pltpu.VMEM((ulysses, FR, local, head), bf16),
            pltpu.VMEM((ulysses, given, local, head), bf16),
            pltpu.VMEM((ulysses, given, local, head), bf16),
            pltpu.SMEM((windows,), jnp.int32),
            pltpu.SMEM((FR,), jnp.int32),
            pltpu.SMEM((FR,), jnp.float32),
            pltpu.SMEM((FR,), jnp.int32),
            pltpu.SMEM((FR,), jnp.float32),
            pltpu.SMEM((windows * share,), jnp.int32),
            pltpu.SMEM((FR,), jnp.int32),
        ]
        + [sems, pltpu.SemaphoreType.DMA((steps, ulysses))]
        + [sems] * 12
        + [pltpu.SemaphoreType.DMA((ulysses,))] * 4
        + [pltpu.SemaphoreType.DMA((CHUNKS,))] * 2,
        compiler_params=pltpu.CompilerParams(
            collective_id=0, has_side_effects=True, vmem_limit_bytes=62 * 1000 * 1000
        ),
    )(
        window_start,
        owner_of_phase,
        blend_weight,
        query_rows.reshape(tokens, features),
        key_rows.reshape(tokens, features),
        value_rows.reshape(tokens, features),
        query_gain.reshape(1, features),
        key_gain.reshape(1, features),
    )
    return (owned, next_rows[None])


def solution(mesh):
    placed = (
        P(("grp", "win"), None, "uly", None),
        P(("grp", "win"), None, "uly", None),
        P(("grp", "win"), None, "uly", None),
        P(),
        P(),
        P("grp"),
        P("grp"),
        P("grp", None),
    )
    return jax.shard_map(
        per_device,
        mesh=mesh,
        in_specs=placed,
        out_specs=(P(("grp", "win"), "uly", None), P(("grp", "win"), None, "uly", None)),
        check_vma=False,
    )
```

```python
import functools
import math

import jax
import jax.numpy as jnp
from jax import lax
from jax.experimental import pallas as pl
from jax.experimental.pallas import tpu as pltpu
from jax.sharding import PartitionSpec as P

HEADS = 40
WF = 16
FR = 12
HALO = WF - FR
SHIFT = FR // 2
AHEAD = HALO + SHIFT
CHUNKS = 4
LAG_BLEND = 1
LAG_RETURN = 1
LAG_LAST = 2
ROWS = 16


def fused(
    dims,
    start_ref,
    owner_ref,
    weight_ref,
    q_ref,
    k_ref,
    v_ref,
    qg_hbm,
    kg_hbm,
    owned_ref,
    next_ref,
    q_now,
    k_now,
    root,
    stage,
    inbox,
    vbox,
    attended,
    halo_in,
    halo_now,
    x_out,
    x_in,
    r_out,
    r_in,
    n_in,
    pool,
    raw_out,
    raw_in,
    blended,
    rl_out,
    rl_in,
    inverse,
    near_at,
    near_w,
    far_at,
    far_w,
    give_at,
    owned_at,
    q_send,
    q_recv,
    k_send,
    k_recv,
    v_send,
    v_recv,
    ho_send,
    ho_recv,
    xo_send,
    xo_recv,
    ro_send,
    ro_recv,
    no_send,
    no_recv,
    raw_send,
    raw_recv,
    n_last,
    r_last,
    q_load,
    k_load,
    qg_ref,
    kg_ref,
    gain_load,
):
    ulysses, windows, share, given, steps, head, tokens = dims
    local = tokens // WF
    me = lax.axis_index("uly")
    my_window = lax.axis_index("win")
    below = lax.rem(my_window + windows - 1, windows)
    above = lax.rem(my_window + 1, windows)

    def peer(d):
        return lax.rem(me + d, ulysses)

    def far(d):
        return lax.rem(my_window + d, windows)

    def near_first(d):
        if ulysses % 2:
            return peer(d)
        pair = lax.rem(lax.div(me, 2) + d // 2, ulysses // 2)
        return pair * 2 + lax.rem(me + d, 2)

    def given_slots(d):
        return (0, 1) if d == 1 else (1 + (d - 2) * share, share)

    chunk = tokens // CHUNKS

    def load(ref, now, sem, c):
        rows = pl.ds(pl.multiple_of(c * chunk, chunk), chunk)
        return pltpu.make_async_copy(ref.at[rows], now.at[rows], sem.at[c])

    for ref, now, sem in ((q_ref, q_now, q_load), (k_ref, k_now, k_load)):
        for c in range(CHUNKS):
            load(ref, now, sem, c).start()

    barrier = pltpu.get_barrier_semaphore()
    for d in range(1, ulysses):
        pl.semaphore_signal(
            barrier, inc=1, device_id={"uly": peer(d)}, device_id_type=pl.DeviceIdType.MESH
        )
    for d in range(1, windows):
        pl.semaphore_signal(
            barrier, inc=1, device_id={"win": far(d)}, device_id_type=pl.DeviceIdType.MESH
        )

    gains = (
        pltpu.make_async_copy(qg_hbm, qg_ref, gain_load.at[0]),
        pltpu.make_async_copy(kg_hbm, kg_ref, gain_load.at[1]),
    )
    for copy in gains:
        copy.start()

    def remote(source, target, send, recv, to):
        pltpu.make_async_remote_copy(
            src_ref=source,
            dst_ref=target,
            send_sem=send,
            recv_sem=recv,
            device_id=to,
            device_id_type=pl.DeviceIdType.MESH,
        ).start()

    def spread(source, target, send, recv):
        for d in range(1, ulysses):
            to = near_first(d)
            remote(source(to), target(me), send, recv, {"uly": to})
        pltpu.make_async_copy(source(me), target(me), recv).start()

    def arrived(ref, sem):
        pltpu.make_async_copy(ref, ref, sem).wait()

    def columns(u, s):
        return pl.ds(pl.multiple_of((u * steps + s) * head, head), head)

    def scale_columns(which, s):
        now, gain = ((q_now, qg_ref), (k_now, kg_ref))[which]
        for u in range(ulysses):
            at = columns(u, s)
            scaled = now[:, at].astype(jnp.float32) * root[which] * gain[:, at]
            stage[which, u, s] = scaled.astype(jnp.bfloat16)

    def send_values(s):
        spread(
            lambda u: v_ref.at[:, columns(u, s)],
            lambda u: vbox.at[s, u],
            v_send.at[s],
            v_recv.at[s],
        )

    def send_scored(which, s):
        spread(
            lambda u: stage.at[which, u, s],
            lambda u: inbox.at[which, s, u],
            (q_send, k_send)[which].at[s],
            q_recv.at[s, me] if which == 0 else k_recv.at[s],
        )

    frames_total = FR * windows

    def tables():
        def invert(o, carry):
            def seek(phase, found):
                return jnp.where(owner_ref[phase] == o, phase, found)

            inverse[o] = lax.fori_loop(0, windows, seek, jnp.int32(0))
            return carry

        lax.fori_loop(0, windows, invert, 0)
        my_phase = inverse[my_window]
        first = FR * my_window + HALO

        def per_owner(o, carry):
            rest = lax.rem(inverse[o] - first + frames_total, windows)
            for c in range(share):
                give_at[o * share + c] = jnp.minimum(rest + c * windows, FR - 1)
            return carry

        lax.fori_loop(0, windows, per_owner, 0)
        rest = lax.rem(inverse[below] - first + frames_total, windows)
        extra = jnp.int32(AHEAD)
        for f in range(AHEAD, FR):
            extra = jnp.where(rest == f % windows, f, extra)
        give_at[below * share] = extra


        def offset_of(w):
            return jnp.clip(start_ref[w] - FR * w, 0, HALO)

        offset = offset_of(my_window)
        offset_below = offset_of(below)
        offset_above = offset_of(above)
        for f in range(FR):
            own = f + HALO - offset
            near_at[f] = own
            near_w[f] = weight_ref[my_window, own].astype(jnp.float32)
            if f < HALO:
                at = f + WF - offset_below
                held = at < WF
                at = jnp.minimum(at, WF - 1)
                far_at[f] = at - FR
                far_w[f] = jnp.where(held, weight_ref[below, at], 0).astype(jnp.float32)
            elif f >= FR - HALO:
                at = f - (FR - HALO) - offset_above
                held = at >= 0
                at = jnp.maximum(at, 0)
                far_at[f] = at + HALO
                far_w[f] = jnp.where(held, weight_ref[above, at], 0).astype(jnp.float32)
        for f in range(FR):
            place = lax.rem(f * windows + my_phase - HALO + frames_total, frames_total)
            home = place // FR
            at = place - home * FR
            apart = lax.rem(home - my_window + windows, windows)
            given_at = FR + AHEAD + 1 + (apart - 2) * share + at // windows
            ahead = FR + jnp.minimum(at, AHEAD)
            owned_at[f] = jnp.where(
                home == my_window, at, jnp.where(home == above, ahead, given_at)
            )
        return offset + SHIFT - HALO

    for which, (ref, now, sem, gain) in enumerate(
        ((q_ref, q_now, q_load, qg_ref), (k_ref, k_now, k_load, kg_ref))
    ):

        def norm_block(t, carry, which=which, ref=ref, now=now, sem=sem, gain=gain):
            blocks = chunk // ROWS

            @pl.when(lax.rem(t, blocks) == 0)
            def _():
                load(ref, now, sem, t // blocks).wait()

            rows = pl.ds(pl.multiple_of(t * ROWS, ROWS), ROWS)
            floats = now[rows, :].astype(jnp.float32)
            mean_square = jnp.mean(floats * floats, axis=-1, keepdims=True)
            root[which, rows, :] = jnp.broadcast_to(
                lax.rsqrt(mean_square + 1e-06), (ROWS, head)
            )
            return carry

        lax.fori_loop(0, tokens // ROWS, norm_block, 0)
        gains[which].wait()
        scale_columns(which, 0)

    pl.semaphore_wait(barrier, ulysses + windows - 2)

    send_scored(1, 0)
    send_values(0)
    send_scored(0, 0)
    for which in range(2):
        scale_columns(which, 1)

    next_at = tables()

    scale = 1.0 / math.sqrt(head) / math.log(2.0)

    def attend(s, then):
        keys = inbox[1, s].reshape(ulysses * tokens, head)
        values = vbox[s].reshape(ulysses * tokens, head)
        for d in range(ulysses):
            u = near_first(d)
            arrived(inbox.at[0, s, u], q_recv.at[s, u])
            scores = lax.dot_general(
                inbox[0, s, u],
                keys,
                (((1,), (1,)), ((), ())),
                preferred_element_type=jnp.float32,
            )
            exponent = jnp.exp2((scores - jnp.max(scores, axis=-1, keepdims=True)) * scale)
            inverse_sum = 1.0 / jnp.sum(exponent, axis=-1, keepdims=True)
            weights = (exponent * inverse_sum).astype(jnp.bfloat16)
            result = jnp.dot(weights, values, preferred_element_type=jnp.float32)
            then(u, result.astype(jnp.bfloat16).reshape(WF, local, head))

    def both_halos(halo_below, halo_above):
        pl.when(my_window > 0)(halo_below)
        halo_above()
        pl.when(my_window == 0)(halo_below)

    def attention(s):
        arrived(inbox.at[1, s], k_recv.at[s])
        arrived(vbox.at[s], v_recv.at[s])
        send_scored(1, s + 1)
        send_values(s + 1)
        send_scored(0, s + 1)

        def keep(u, result):
            attended[s, u] = result

            def send(side, at, to):
                return lambda: remote(
                    attended.at[s, u, pl.ds(at, HALO)],
                    halo_in.at[s, u, pl.ds(side * HALO, HALO)],
                    ho_send.at[s],
                    ho_recv.at[s],
                    {"win": to},
                )

            both_halos(send(1, 0, below), send(0, FR, above))

        attend(s, keep)

        @pl.when(s + 2 < steps)
        def _():
            for which in range(2):
                scale_columns(which, s + 2)

    def blend(s):
        arrived(halo_in.at[s], ho_recv.at[s])
        for d in range(ulysses):
            u = near_first(ulysses - 1 - d)
            for f in range(2 * HALO):
                halo_now[f, 0] = halo_in[s, u, f]
            for f in range(FR):
                numerator = near_w[f] * attended[s, u, near_at[f]].astype(jnp.float32)
                denominator = near_w[f]
                if f < HALO or f >= FR - HALO:
                    numerator += far_w[f] * halo_now[far_at[f], 0].astype(jnp.float32)
                    denominator += far_w[f]
                x_out[s, u, f] = (numerator / denominator).astype(jnp.bfloat16)
            if d < ulysses - 1:
                remote(x_out.at[s, u], x_in.at[s, me], xo_send.at[s], xo_recv.at[s], {"uly": u})
            else:
                pltpu.make_async_copy(x_out.at[s, u], x_in.at[s, me], xo_recv.at[s]).start()

    def to_all(give):
        for d in range(windows - 1, 0, -1):

            @pl.when(my_window + d < windows)
            def _(d=d):
                give(my_window + d, windows - d)

            @pl.when(my_window >= d)
            def _(d=d):
                give(my_window - d, d)

    def give_back(s):
        arrived(x_in.at[s], xo_recv.at[s])
        for f in range(FR):
            pool[f] = x_in[s, :, f]

        def give(o, apart):
            base, count = given_slots(apart)
            for c in range(count):
                r_out[s, base + c] = pool[give_at[o * share + c]]
            many = pl.ds(base, count)
            remote(
                r_out.at[s, many], r_in.at[s, many], ro_send.at[s], ro_recv.at[s], {"win": o}
            )
            if apart == 1:
                remote(
                    x_in.at[s, :, pl.ds(0, AHEAD)],
                    n_in.at[s],
                    no_send.at[s],
                    no_recv.at[s],
                    {"win": o},
                )

        to_all(give)

    def finish(s):
        arrived(n_in.at[s], no_recv.at[s])
        arrived(r_in.at[s], ro_recv.at[s])
        for f in range(FR):
            pool[f] = x_in[s, :, f]
        for f in range(AHEAD):
            pool[FR + f] = n_in[s, :, f]
        for c in range(given):
            pool[FR + AHEAD + c] = r_in[s, c]
        for f in range(FR):
            frame = pool[owned_at[f]]
            for u in range(ulysses):
                owned_ref[f, :, columns(u, s)] = frame[u]
        for j in range(WF):
            frame = pool[next_at + j]
            for u in range(ulysses):
                next_ref[j, :, columns(u, s)] = frame[u]

    last = steps - 1

    def last_attention():
        arrived(inbox.at[1, last], k_recv.at[last])
        arrived(vbox.at[last], v_recv.at[last])

        def give_raw(u, result):
            raw_out[u] = result

            def send(side, at, to):
                return lambda: remote(
                    raw_out.at[u, pl.ds(at, HALO)],
                    raw_in.at[me, pl.ds(FR + side * HALO, HALO)],
                    raw_send.at[u],
                    raw_recv.at[me],
                    {"win": to, "uly": u},
                )

            both_halos(send(1, 0, below), send(0, FR, above))
            for f in range(FR):
                x_out[last, u, f] = raw_out[u, near_at[f]]
            home = raw_in.at[me, pl.ds(0, FR)]

            @pl.when(u != me)
            def _():
                remote(x_out.at[last, u], home, xo_send.at[last], raw_recv.at[me], {"uly": u})

            @pl.when(u == me)
            def _():
                pltpu.make_async_copy(x_out.at[last, u], home, raw_recv.at[me]).start()

        attend(last, give_raw)

    def last_blend():
        for d in range(ulysses):
            m = near_first(d)
            arrived(raw_in.at[m], raw_recv.at[m])
            for f in range(2 * HALO):
                halo_now[f, 0] = raw_in[m, FR + f]
            for f in range(FR):
                numerator = near_w[f] * raw_in[m, f].astype(jnp.float32)
                denominator = near_w[f]
                if f < HALO or f >= FR - HALO:
                    numerator += far_w[f] * halo_now[far_at[f], 0].astype(jnp.float32)
                    denominator += far_w[f]
                blended[m, f] = (numerator / denominator).astype(jnp.bfloat16)

            def give(o, apart):
                base, count = given_slots(apart)
                for c in range(count):
                    rl_out[m, base + c] = blended[m, give_at[o * share + c]]
                many = pl.ds(base, count)
                remote(
                    rl_out.at[m, many],
                    rl_in.at[m, many],
                    ro_send.at[last],
                    r_last.at[m],
                    {"win": o},
                )
                if apart == 1:
                    remote(
                        blended.at[m, pl.ds(0, AHEAD)],
                        n_in.at[last, m],
                        no_send.at[last],
                        n_last.at[m],
                        {"win": o},
                    )

            to_all(give)

    def last_finish():
        for d in range(ulysses):
            m = near_first(d)
            arrived(n_in.at[last, m], n_last.at[m])
            arrived(rl_in.at[m], r_last.at[m])
            for f in range(FR):
                pool[f, 0] = blended[m, f]
            for f in range(AHEAD):
                pool[FR + f, 0] = n_in[last, m, f]
            for c in range(given):
                pool[FR + AHEAD + c, 0] = rl_in[m, c]
            at = columns(m, last)
            for f in range(FR):
                owned_ref[f, :, at] = pool[owned_at[f], 0]
            for j in range(WF):
                next_ref[j, :, at] = pool[next_at + j, 0]

    def step(i, carry):
        for lag, work in (
            (LAG_BLEND, blend),
            (0, attention),
            (LAG_RETURN, give_back),
            (LAG_LAST, finish),
        ):

            @pl.when((i >= lag) & (i < last + lag))
            def _(lag=lag, work=work):
                work(i - lag)

        return carry

    lax.fori_loop(0, last, step, 0)
    blend(last - 1)
    last_attention()
    give_back(last - 1)
    last_blend()
    finish(last - 2)
    finish(last - 1)
    last_finish()

    def sent(s, carry):
        arrived(inbox.at[0, s, pl.ds(0, ulysses - 1)], q_send.at[s])
        arrived(inbox.at[1, s, pl.ds(0, ulysses - 1)], k_send.at[s])
        arrived(vbox.at[s, pl.ds(0, ulysses - 1)], v_send.at[s])
        arrived(x_out.at[s, pl.ds(0, ulysses - 1)], xo_send.at[s])
        arrived(n_in.at[s], no_send.at[s])
        arrived(r_in.at[s], ro_send.at[s])
        return carry

    lax.fori_loop(0, steps, sent, 0)

    def halo_sent(s, carry):
        arrived(halo_in.at[s], ho_send.at[s])
        return carry

    lax.fori_loop(0, last, halo_sent, 0)
    for u in range(ulysses):
        arrived(raw_in.at[u, pl.ds(FR, 2 * HALO)], raw_send.at[u])


def per_device(
    query_rows,
    key_rows,
    value_rows,
    query_gain,
    key_gain,
    window_start,
    owner_of_phase,
    blend_weight,
):
    windows = lax.axis_size("win")
    ulysses = lax.axis_size("uly")
    share = (FR + windows - 1) // windows
    given = 1 + (windows - 2) * share
    local = query_rows.shape[2]
    features = query_rows.shape[3]
    head = features // HEADS
    steps = HEADS // ulysses
    tokens = WF * local
    smem = pl.BlockSpec(memory_space=pltpu.SMEM)
    vmem = pl.BlockSpec(memory_space=pltpu.VMEM)
    hbm = pl.BlockSpec(memory_space=pl.ANY)
    bf16 = jnp.bfloat16
    sems = pltpu.SemaphoreType.DMA((steps,))
    frame = (ulysses, local, head)
    owned, next_rows = pl.pallas_call(
        functools.partial(fused, (ulysses, windows, share, given, steps, head, tokens)),
        out_shape=(
            pltpu.VMEM((FR, local, features), bf16),
            pltpu.VMEM((WF, local, features), bf16),
        ),
        in_specs=[smem] * 3 + [hbm] * 5,
        out_specs=(vmem, vmem),
        scratch_shapes=[
            pltpu.VMEM((tokens, features), bf16),
            pltpu.VMEM((tokens, features), bf16),
            pltpu.VMEM((2, tokens, head), jnp.float32),
            pltpu.VMEM((2, ulysses, steps, tokens, head), bf16),
            pltpu.VMEM((2, steps, ulysses, tokens, head), bf16),
            pltpu.VMEM((steps, ulysses, tokens, head), bf16),
            pltpu.VMEM((steps, ulysses, WF, local, head), bf16),
            pltpu.VMEM((steps, ulysses, 2 * HALO, local, head), bf16),
            pltpu.VMEM((2 * HALO,) + frame, bf16),
            pltpu.VMEM((steps, ulysses, FR, local, head), bf16),
            pltpu.VMEM((steps, ulysses, FR, local, head), bf16),
            pltpu.VMEM((steps, given) + frame, bf16),
            pltpu.VMEM((steps, given) + frame, bf16),
            pltpu.VMEM((steps, ulysses, AHEAD, local, head), bf16),
            pltpu.VMEM((FR + AHEAD + given,) + frame, bf16),
            pltpu.VMEM((ulysses, WF, local, head), bf16),
            pltpu.VMEM((ulysses, FR + 2 * HALO, local, head), bf16),
            pltpu.VMEM((ulysses, FR, local, head), bf16),
            pltpu.VMEM((ulysses, given, local, head), bf16),
            pltpu.VMEM((ulysses, given, local, head), bf16),
            pltpu.SMEM((windows,), jnp.int32),
            pltpu.SMEM((FR,), jnp.int32),
            pltpu.SMEM((FR,), jnp.float32),
            pltpu.SMEM((FR,), jnp.int32),
            pltpu.SMEM((FR,), jnp.float32),
            pltpu.SMEM((windows * share,), jnp.int32),
            pltpu.SMEM((FR,), jnp.int32),
        ]
        + [sems, pltpu.SemaphoreType.DMA((steps, ulysses))]
        + [sems] * 12
        + [pltpu.SemaphoreType.DMA((ulysses,))] * 4
        + [pltpu.SemaphoreType.DMA((CHUNKS,))] * 2
        + [pltpu.VMEM((1, features), jnp.float32)] * 2
        + [pltpu.SemaphoreType.DMA((2,))],
        compiler_params=pltpu.CompilerParams(
            collective_id=0, has_side_effects=True, vmem_limit_bytes=62 * 1000 * 1000
        ),
    )(
        window_start,
        owner_of_phase,
        blend_weight,
        query_rows.reshape(tokens, features),
        key_rows.reshape(tokens, features),
        value_rows.reshape(tokens, features),
        query_gain.reshape(1, features),
        key_gain.reshape(1, features),
    )
    return (owned, next_rows[None])


def solution(mesh):
    placed = (
        P(("grp", "win"), None, "uly", None),
        P(("grp", "win"), None, "uly", None),
        P(("grp", "win"), None, "uly", None),
        P(),
        P(),
        P("grp"),
        P("grp"),
        P("grp", None),
    )
    return jax.shard_map(
        per_device,
        mesh=mesh,
        in_specs=placed,
        out_specs=(P(("grp", "win"), "uly", None), P(("grp", "win"), None, "uly", None)),
        check_vma=False,
    )
```

```python
import functools
import math

import jax
import jax.numpy as jnp
from jax import lax
from jax.experimental import pallas as pl
from jax.experimental.pallas import tpu as pltpu
from jax.sharding import PartitionSpec as P

HEADS = 40
WF = 16
FR = 12
HALO = WF - FR
SHIFT = FR // 2
AHEAD = HALO + SHIFT
CHUNKS = 4
LAG_BLEND = 1
LAG_RETURN = 1
LAG_LAST = 3
ROWS = 16


def fused(
    dims,
    start_ref,
    owner_ref,
    weight_ref,
    q_ref,
    k_ref,
    v_ref,
    qg_hbm,
    kg_hbm,
    owned_ref,
    next_ref,
    q_now,
    k_now,
    root,
    stage,
    inbox,
    vbox,
    attended,
    halo_in,
    halo_now,
    x_out,
    x_in,
    r_out,
    r_in,
    n_in,
    pool,
    raw_out,
    raw_in,
    blended,
    rl_out,
    rl_in,
    inverse,
    near_at,
    near_w,
    far_at,
    far_w,
    give_at,
    owned_at,
    q_send,
    q_recv,
    k_send,
    k_recv,
    v_send,
    v_recv,
    ho_send,
    ho_recv,
    xo_send,
    xo_recv,
    ro_send,
    ro_recv,
    no_send,
    no_recv,
    raw_send,
    raw_recv,
    n_last,
    r_last,
    q_load,
    k_load,
    qg_ref,
    kg_ref,
    gain_load,
):
    ulysses, windows, share, given, steps, head, tokens = dims
    local = tokens // WF
    me = lax.axis_index("uly")
    my_window = lax.axis_index("win")
    below = lax.rem(my_window + windows - 1, windows)
    above = lax.rem(my_window + 1, windows)

    def peer(d):
        return lax.rem(me + d, ulysses)

    def far(d):
        return lax.rem(my_window + d, windows)

    def near_first(d):
        if ulysses % 2:
            return peer(d)
        pair = lax.rem(lax.div(me, 2) + d // 2, ulysses // 2)
        return pair * 2 + lax.rem(me + d, 2)

    def given_slots(d):
        return (0, 1) if d == 1 else (1 + (d - 2) * share, share)

    chunk = tokens // CHUNKS

    def load(ref, now, sem, c):
        rows = pl.ds(pl.multiple_of(c * chunk, chunk), chunk)
        return pltpu.make_async_copy(ref.at[rows], now.at[rows], sem.at[c])

    for ref, now, sem in ((q_ref, q_now, q_load), (k_ref, k_now, k_load)):
        for c in range(CHUNKS):
            load(ref, now, sem, c).start()

    barrier = pltpu.get_barrier_semaphore()
    for d in range(1, ulysses):
        pl.semaphore_signal(
            barrier, inc=1, device_id={"uly": peer(d)}, device_id_type=pl.DeviceIdType.MESH
        )
    for d in range(1, windows):
        pl.semaphore_signal(
            barrier, inc=1, device_id={"win": far(d)}, device_id_type=pl.DeviceIdType.MESH
        )

    gains = (
        pltpu.make_async_copy(qg_hbm, qg_ref, gain_load.at[0]),
        pltpu.make_async_copy(kg_hbm, kg_ref, gain_load.at[1]),
    )
    for copy in gains:
        copy.start()

    def remote(source, target, send, recv, to):
        pltpu.make_async_remote_copy(
            src_ref=source,
            dst_ref=target,
            send_sem=send,
            recv_sem=recv,
            device_id=to,
            device_id_type=pl.DeviceIdType.MESH,
        ).start()

    def spread(source, target, send, recv):
        for d in range(1, ulysses):
            to = near_first(d)
            remote(source(to), target(me), send, recv, {"uly": to})
        pltpu.make_async_copy(source(me), target(me), recv).start()

    def arrived(ref, sem):
        pltpu.make_async_copy(ref, ref, sem).wait()

    def columns(u, s):
        return pl.ds(pl.multiple_of((u * steps + s) * head, head), head)

    def scale_columns(which, s):
        now, gain = ((q_now, qg_ref), (k_now, kg_ref))[which]
        for u in range(ulysses):
            at = columns(u, s)
            scaled = now[:, at].astype(jnp.float32) * root[which] * gain[:, at]
            stage[which, u, s] = scaled.astype(jnp.bfloat16)

    def send_values(s):
        spread(
            lambda u: v_ref.at[:, columns(u, s)],
            lambda u: vbox.at[s, u],
            v_send.at[s],
            v_recv.at[s],
        )

    def send_scored(which, s):
        spread(
            lambda u: stage.at[which, u, s],
            lambda u: inbox.at[which, s, u],
            (q_send, k_send)[which].at[s],
            q_recv.at[s, me] if which == 0 else k_recv.at[s],
        )

    frames_total = FR * windows

    def tables():
        def invert(o, carry):
            def seek(phase, found):
                return jnp.where(owner_ref[phase] == o, phase, found)

            inverse[o] = lax.fori_loop(0, windows, seek, jnp.int32(0))
            return carry

        lax.fori_loop(0, windows, invert, 0)
        my_phase = inverse[my_window]
        first = FR * my_window + HALO

        def per_owner(o, carry):
            rest = lax.rem(inverse[o] - first + frames_total, windows)
            for c in range(share):
                give_at[o * share + c] = jnp.minimum(rest + c * windows, FR - 1)
            return carry

        lax.fori_loop(0, windows, per_owner, 0)
        rest = lax.rem(inverse[below] - first + frames_total, windows)
        extra = jnp.int32(AHEAD)
        for f in range(AHEAD, FR):
            extra = jnp.where(rest == f % windows, f, extra)
        give_at[below * share] = extra


        def offset_of(w):
            return jnp.clip(start_ref[w] - FR * w, 0, HALO)

        offset = offset_of(my_window)
        offset_below = offset_of(below)
        offset_above = offset_of(above)
        for f in range(FR):
            own = f + HALO - offset
            near_at[f] = own
            near_w[f] = weight_ref[my_window, own].astype(jnp.float32)
            if f < HALO:
                at = f + WF - offset_below
                held = at < WF
                at = jnp.minimum(at, WF - 1)
                far_at[f] = at - FR
                far_w[f] = jnp.where(held, weight_ref[below, at], 0).astype(jnp.float32)
            elif f >= FR - HALO:
                at = f - (FR - HALO) - offset_above
                held = at >= 0
                at = jnp.maximum(at, 0)
                far_at[f] = at + HALO
                far_w[f] = jnp.where(held, weight_ref[above, at], 0).astype(jnp.float32)
        for f in range(FR):
            place = lax.rem(f * windows + my_phase - HALO + frames_total, frames_total)
            home = place // FR
            at = place - home * FR
            apart = lax.rem(home - my_window + windows, windows)
            given_at = FR + AHEAD + 1 + (apart - 2) * share + at // windows
            ahead = FR + jnp.minimum(at, AHEAD)
            owned_at[f] = jnp.where(
                home == my_window, at, jnp.where(home == above, ahead, given_at)
            )
        return offset + SHIFT - HALO

    for which, (ref, now, sem, gain) in enumerate(
        ((q_ref, q_now, q_load, qg_ref), (k_ref, k_now, k_load, kg_ref))
    ):

        def norm_block(t, carry, which=which, ref=ref, now=now, sem=sem, gain=gain):
            blocks = chunk // ROWS

            @pl.when(lax.rem(t, blocks) == 0)
            def _():
                load(ref, now, sem, t // blocks).wait()

            rows = pl.ds(pl.multiple_of(t * ROWS, ROWS), ROWS)
            floats = now[rows, :].astype(jnp.float32)
            mean_square = jnp.mean(floats * floats, axis=-1, keepdims=True)
            root[which, rows, :] = jnp.broadcast_to(
                lax.rsqrt(mean_square + 1e-06), (ROWS, head)
            )
            return carry

        lax.fori_loop(0, tokens // ROWS, norm_block, 0)
        gains[which].wait()
        scale_columns(which, 0)

    pl.semaphore_wait(barrier, ulysses + windows - 2)

    send_scored(1, 0)
    send_values(0)
    send_scored(0, 0)
    for which in range(2):
        scale_columns(which, 1)

    next_at = tables()

    scale = 1.0 / math.sqrt(head) / math.log(2.0)

    def attend(s, then):
        keys = inbox[1, s].reshape(ulysses * tokens, head)
        values = vbox[s].reshape(ulysses * tokens, head)
        for d in range(ulysses):
            u = near_first(d)
            arrived(inbox.at[0, s, u], q_recv.at[s, u])
            scores = lax.dot_general(
                inbox[0, s, u],
                keys,
                (((1,), (1,)), ((), ())),
                preferred_element_type=jnp.float32,
            )
            exponent = jnp.exp2((scores - jnp.max(scores, axis=-1, keepdims=True)) * scale)
            inverse_sum = 1.0 / jnp.sum(exponent, axis=-1, keepdims=True)
            weights = (exponent * inverse_sum).astype(jnp.bfloat16)
            result = jnp.dot(weights, values, preferred_element_type=jnp.float32)
            then(u, result.astype(jnp.bfloat16).reshape(WF, local, head))

    def both_halos(halo_below, halo_above):
        pl.when(my_window > 0)(halo_below)
        halo_above()
        pl.when(my_window == 0)(halo_below)

    def attention(s):
        arrived(inbox.at[1, s], k_recv.at[s])
        arrived(vbox.at[s], v_recv.at[s])
        send_scored(1, s + 1)
        send_values(s + 1)
        send_scored(0, s + 1)

        def keep(u, result):
            attended[s, u] = result

            def send(side, at, to):
                return lambda: remote(
                    attended.at[s, u, pl.ds(at, HALO)],
                    halo_in.at[s, u, pl.ds(side * HALO, HALO)],
                    ho_send.at[s],
                    ho_recv.at[s],
                    {"win": to},
                )

            both_halos(send(1, 0, below), send(0, FR, above))

        attend(s, keep)

    def blend(s):
        arrived(halo_in.at[s], ho_recv.at[s])
        for d in range(ulysses):
            u = near_first(ulysses - 1 - d)
            for f in range(2 * HALO):
                halo_now[f, 0] = halo_in[s, u, f]
            for f in range(FR):
                numerator = near_w[f] * attended[s, u, near_at[f]].astype(jnp.float32)
                denominator = near_w[f]
                if f < HALO or f >= FR - HALO:
                    numerator += far_w[f] * halo_now[far_at[f], 0].astype(jnp.float32)
                    denominator += far_w[f]
                x_out[s, u, f] = (numerator / denominator).astype(jnp.bfloat16)
            if d < ulysses - 1:
                remote(x_out.at[s, u], x_in.at[s, me], xo_send.at[s], xo_recv.at[s], {"uly": u})
            else:
                pltpu.make_async_copy(x_out.at[s, u], x_in.at[s, me], xo_recv.at[s]).start()

    def to_all(give):
        for d in range(windows - 1, 0, -1):

            @pl.when(my_window + d < windows)
            def _(d=d):
                give(my_window + d, windows - d)

            @pl.when(my_window >= d)
            def _(d=d):
                give(my_window - d, d)

    def give_back(s):
        arrived(x_in.at[s], xo_recv.at[s])
        for f in range(FR):
            pool[f] = x_in[s, :, f]

        def give(o, apart):
            base, count = given_slots(apart)
            for c in range(count):
                r_out[s, base + c] = pool[give_at[o * share + c]]
            many = pl.ds(base, count)
            remote(
                r_out.at[s, many], r_in.at[s, many], ro_send.at[s], ro_recv.at[s], {"win": o}
            )
            if apart == 1:
                remote(
                    x_in.at[s, :, pl.ds(0, AHEAD)],
                    n_in.at[s],
                    no_send.at[s],
                    no_recv.at[s],
                    {"win": o},
                )

        to_all(give)

    def finish(s):
        arrived(n_in.at[s], no_recv.at[s])
        arrived(r_in.at[s], ro_recv.at[s])
        for f in range(FR):
            pool[f] = x_in[s, :, f]
        for f in range(AHEAD):
            pool[FR + f] = n_in[s, :, f]
        for c in range(given):
            pool[FR + AHEAD + c] = r_in[s, c]
        for f in range(FR):
            frame = pool[owned_at[f]]
            for u in range(ulysses):
                owned_ref[f, :, columns(u, s)] = frame[u]
        for j in range(WF):
            frame = pool[next_at + j]
            for u in range(ulysses):
                next_ref[j, :, columns(u, s)] = frame[u]

    last = steps - 1

    def last_attention():
        arrived(inbox.at[1, last], k_recv.at[last])
        arrived(vbox.at[last], v_recv.at[last])

        def give_raw(u, result):
            raw_out[u] = result

            def send(side, at, to):
                return lambda: remote(
                    raw_out.at[u, pl.ds(at, HALO)],
                    raw_in.at[me, pl.ds(FR + side * HALO, HALO)],
                    raw_send.at[u],
                    raw_recv.at[me],
                    {"win": to, "uly": u},
                )

            both_halos(send(1, 0, below), send(0, FR, above))
            for f in range(FR):
                x_out[last, u, f] = raw_out[u, near_at[f]]
            home = raw_in.at[me, pl.ds(0, FR)]

            @pl.when(u != me)
            def _():
                remote(x_out.at[last, u], home, xo_send.at[last], raw_recv.at[me], {"uly": u})

            @pl.when(u == me)
            def _():
                pltpu.make_async_copy(x_out.at[last, u], home, raw_recv.at[me]).start()

        attend(last, give_raw)

    def last_blend():
        for d in range(ulysses):
            m = near_first(d)
            arrived(raw_in.at[m], raw_recv.at[m])
            for f in range(2 * HALO):
                halo_now[f, 0] = raw_in[m, FR + f]
            for f in range(FR):
                numerator = near_w[f] * raw_in[m, f].astype(jnp.float32)
                denominator = near_w[f]
                if f < HALO or f >= FR - HALO:
                    numerator += far_w[f] * halo_now[far_at[f], 0].astype(jnp.float32)
                    denominator += far_w[f]
                blended[m, f] = (numerator / denominator).astype(jnp.bfloat16)

            def give(o, apart):
                base, count = given_slots(apart)
                for c in range(count):
                    rl_out[m, base + c] = blended[m, give_at[o * share + c]]
                many = pl.ds(base, count)
                remote(
                    rl_out.at[m, many],
                    rl_in.at[m, many],
                    ro_send.at[last],
                    r_last.at[m],
                    {"win": o},
                )
                if apart == 1:
                    remote(
                        blended.at[m, pl.ds(0, AHEAD)],
                        n_in.at[last, m],
                        no_send.at[last],
                        n_last.at[m],
                        {"win": o},
                    )

            to_all(give)

    def last_finish():
        for d in range(ulysses):
            m = near_first(d)
            arrived(n_in.at[last, m], n_last.at[m])
            arrived(rl_in.at[m], r_last.at[m])
            for f in range(FR):
                pool[f, 0] = blended[m, f]
            for f in range(AHEAD):
                pool[FR + f, 0] = n_in[last, m, f]
            for c in range(given):
                pool[FR + AHEAD + c, 0] = rl_in[m, c]
            at = columns(m, last)
            for f in range(FR):
                owned_ref[f, :, at] = pool[owned_at[f], 0]
            for j in range(WF):
                next_ref[j, :, at] = pool[next_at + j, 0]

    def step(i, carry):
        for lag, work in (
            (LAG_BLEND, blend),
            (0, attention),
            (LAG_RETURN, give_back),
            (LAG_LAST, finish),
        ):

            @pl.when((i >= lag) & (i < last + lag))
            def _(lag=lag, work=work):
                work(i - lag)

        @pl.when(i + 2 < steps)
        def _():
            for which in range(2):
                scale_columns(which, i + 2)

        return carry

    lax.fori_loop(0, last, step, 0)
    blend(last - 1)
    last_attention()
    give_back(last - 1)
    finish(last - 3)
    last_blend()
    finish(last - 2)
    finish(last - 1)
    last_finish()

    def sent(s, carry):
        arrived(inbox.at[0, s, pl.ds(0, ulysses - 1)], q_send.at[s])
        arrived(inbox.at[1, s, pl.ds(0, ulysses - 1)], k_send.at[s])
        arrived(vbox.at[s, pl.ds(0, ulysses - 1)], v_send.at[s])
        arrived(x_out.at[s, pl.ds(0, ulysses - 1)], xo_send.at[s])
        arrived(n_in.at[s], no_send.at[s])
        arrived(r_in.at[s], ro_send.at[s])
        return carry

    lax.fori_loop(0, steps, sent, 0)

    def halo_sent(s, carry):
        arrived(halo_in.at[s], ho_send.at[s])
        return carry

    lax.fori_loop(0, last, halo_sent, 0)
    for u in range(ulysses):
        arrived(raw_in.at[u, pl.ds(FR, 2 * HALO)], raw_send.at[u])


def per_device(
    query_rows,
    key_rows,
    value_rows,
    query_gain,
    key_gain,
    window_start,
    owner_of_phase,
    blend_weight,
):
    windows = lax.axis_size("win")
    ulysses = lax.axis_size("uly")
    share = (FR + windows - 1) // windows
    given = 1 + (windows - 2) * share
    local = query_rows.shape[2]
    features = query_rows.shape[3]
    head = features // HEADS
    steps = HEADS // ulysses
    tokens = WF * local
    smem = pl.BlockSpec(memory_space=pltpu.SMEM)
    vmem = pl.BlockSpec(memory_space=pltpu.VMEM)
    hbm = pl.BlockSpec(memory_space=pl.ANY)
    bf16 = jnp.bfloat16
    sems = pltpu.SemaphoreType.DMA((steps,))
    frame = (ulysses, local, head)
    owned, next_rows = pl.pallas_call(
        functools.partial(fused, (ulysses, windows, share, given, steps, head, tokens)),
        out_shape=(
            pltpu.VMEM((FR, local, features), bf16),
            pltpu.VMEM((WF, local, features), bf16),
        ),
        in_specs=[smem] * 3 + [hbm] * 5,
        out_specs=(vmem, vmem),
        scratch_shapes=[
            pltpu.VMEM((tokens, features), bf16),
            pltpu.VMEM((tokens, features), bf16),
            pltpu.VMEM((2, tokens, head), jnp.float32),
            pltpu.VMEM((2, ulysses, steps, tokens, head), bf16),
            pltpu.VMEM((2, steps, ulysses, tokens, head), bf16),
            pltpu.VMEM((steps, ulysses, tokens, head), bf16),
            pltpu.VMEM((steps, ulysses, WF, local, head), bf16),
            pltpu.VMEM((steps, ulysses, 2 * HALO, local, head), bf16),
            pltpu.VMEM((2 * HALO,) + frame, bf16),
            pltpu.VMEM((steps, ulysses, FR, local, head), bf16),
            pltpu.VMEM((steps, ulysses, FR, local, head), bf16),
            pltpu.VMEM((steps, given) + frame, bf16),
            pltpu.VMEM((steps, given) + frame, bf16),
            pltpu.VMEM((steps, ulysses, AHEAD, local, head), bf16),
            pltpu.VMEM((FR + AHEAD + given,) + frame, bf16),
            pltpu.VMEM((ulysses, WF, local, head), bf16),
            pltpu.VMEM((ulysses, FR + 2 * HALO, local, head), bf16),
            pltpu.VMEM((ulysses, FR, local, head), bf16),
            pltpu.VMEM((ulysses, given, local, head), bf16),
            pltpu.VMEM((ulysses, given, local, head), bf16),
            pltpu.SMEM((windows,), jnp.int32),
            pltpu.SMEM((FR,), jnp.int32),
            pltpu.SMEM((FR,), jnp.float32),
            pltpu.SMEM((FR,), jnp.int32),
            pltpu.SMEM((FR,), jnp.float32),
            pltpu.SMEM((windows * share,), jnp.int32),
            pltpu.SMEM((FR,), jnp.int32),
        ]
        + [sems, pltpu.SemaphoreType.DMA((steps, ulysses))]
        + [sems] * 12
        + [pltpu.SemaphoreType.DMA((ulysses,))] * 4
        + [pltpu.SemaphoreType.DMA((CHUNKS,))] * 2
        + [pltpu.VMEM((1, features), jnp.float32)] * 2
        + [pltpu.SemaphoreType.DMA((2,))],
        compiler_params=pltpu.CompilerParams(
            collective_id=0, has_side_effects=True, vmem_limit_bytes=62 * 1000 * 1000
        ),
    )(
        window_start,
        owner_of_phase,
        blend_weight,
        query_rows.reshape(tokens, features),
        key_rows.reshape(tokens, features),
        value_rows.reshape(tokens, features),
        query_gain.reshape(1, features),
        key_gain.reshape(1, features),
    )
    return (owned, next_rows[None])


def solution(mesh):
    placed = (
        P(("grp", "win"), None, "uly", None),
        P(("grp", "win"), None, "uly", None),
        P(("grp", "win"), None, "uly", None),
        P(),
        P(),
        P("grp"),
        P("grp"),
        P("grp", None),
    )
    return jax.shard_map(
        per_device,
        mesh=mesh,
        in_specs=placed,
        out_specs=(P(("grp", "win"), "uly", None), P(("grp", "win"), None, "uly", None)),
        check_vma=False,
    )
```
